32 devices in a mesh: row: 4 (over y, core), col: 8 (over z, x).
Axes of the slice: x: 2, y: 2, z: 4, core: 2. Of those that a mesh axis runs over, the one named last changes fastest.
Arguments:
- positions: float32 [3, 512], P(None, ('row', 'col')), as said below
- thermal_noise: float32 [32, 3, 512], P(None, None, ('row', 'col')), as said below
Outputs:
- displacement: float32 [32, 3, 512], P(None, None, ('row', 'col'))
Inputs may be any that keep to these rules, and one draw needn't show every extreme that they name: `positions`: any two particles are at least 1.0 apart. `thermal_noise`: finite real entries.
All inputs are finite; a program needn't handle non-finite values.
Results may differ from the reference program's by a relative error of at most 0.0013.
Values may be sent and summed in bfloat16 or wider, within the bound.
A program may use at most 64 MiB of HBM per device.

```python
import math
import jax
import jax.numpy as jnp
from jax import lax

SAMPLES = 32
PARTICLES = 512


def draw_positions(key, part):
    lattice_side = 1
    while lattice_side ** 3 < PARTICLES:
        lattice_side = lattice_side + 1
    cells = jax.random.permutation(jax.random.fold_in(key, 11), lattice_side ** 3)[:PARTICLES]
    lattice = jnp.stack([cells // (lattice_side * lattice_side), cells // lattice_side % lattice_side, cells % lattice_side]).astype(jnp.float32)
    jitter = jax.random.uniform(jax.random.fold_in(key, 14), (3, PARTICLES), jnp.float32, -0.3, 0.3)
    return (2.5 * (lattice + jitter)).astype(jnp.float32)


def draw_thermal_noise(key, part):
    ramp = jnp.arange(PARTICLES, dtype=jnp.float32) / PARTICLES
    gaussian = jax.random.normal(jax.random.fold_in(key, 21), (SAMPLES, 3, PARTICLES), jnp.float32)
    return (gaussian * jnp.exp(0.5 * ramp * math.log(3.0))).astype(jnp.float32)


def setup_inputs(seed: int = 0) -> dict:
    key_list = jax.random.split(jax.random.key(seed), 3)
    return {
        "positions": draw_positions(jax.random.fold_in(key_list[2], 71), 0),
        "thermal_noise": draw_thermal_noise(jax.random.fold_in(key_list[2], 71), 0),
    }


def pair_tensor(rows_pos, cols_pos, retain):
    offsets = [rows_pos[a][None, :] - cols_pos[a][:, None] for a in range(3)]
    squared = offsets[0] * offsets[0] + offsets[1] * offsets[1] + offsets[2] * offsets[2]
    guarded = jnp.where(retain, squared, 4.0)
    inverse = lax.rsqrt(guarded)
    distance = guarded * inverse
    correlation = distance < 2.0
    inverse_cube = inverse * inverse * inverse
    inverse_fifth = inverse_cube * inverse * inverse
    isotropic = jnp.where(correlation, 1.0 - 0.28125 * distance, 0.75 * inverse + 0.5 * inverse_cube)
    dyadic = jnp.where(correlation, 0.09375 * inverse, 0.75 * inverse_cube - 1.5 * inverse_fifth)
    isotropic = jnp.where(retain, isotropic, 0.0)
    dyadic = jnp.where(retain, dyadic, 0.0)
    columns = []
    for b in range(3):
        elements = []
        for a in range(3):
            element = dyadic * offsets[a] * offsets[b]
            if a == b:
                element = element + isotropic
            elements.append(element)
        columns.append(jnp.stack(elements, axis=1))
    return jnp.stack(columns, axis=0)

def apply_mobility(positions, vector):
    particles = positions.shape[1]
    block_rows = 128
    rounded = vector.astype(jnp.bfloat16)
    rounded = lax.optimization_barrier(rounded).astype(jnp.float32)

    def one_block(row_start):
        rows_pos = lax.dynamic_slice_in_dim(positions, row_start, block_rows, 1)
        row_label = row_start + jnp.arange(block_rows, dtype=jnp.int32)
        col_label = jnp.arange(particles, dtype=jnp.int32)
        retain = row_label[None, :] != col_label[:, None]
        tensor = pair_tensor(rows_pos, positions, retain).astype(jnp.bfloat16)
        tensor = lax.optimization_barrier(tensor).astype(jnp.float32)
        return jnp.einsum('kbj,bjai->kai', rounded, tensor, precision=lax.Precision.HIGHEST)
    block_starts = jnp.arange(particles // block_rows, dtype=jnp.int32) * block_rows
    block_terms = lax.map(one_block, block_starts)
    coupled = jnp.transpose(block_terms, (1, 2, 0, 3)).reshape(vector.shape)
    return vector + coupled

def reference(positions, thermal_noise):
    squares = lax.optimization_barrier(jnp.sum(thermal_noise * thermal_noise, axis=(1, 2)))
    noise_length = jnp.sqrt(squares + 1e-06)
    basis_one = thermal_noise / noise_length[:, None, None]
    image_one = apply_mobility(positions, basis_one)
    alpha_one = lax.optimization_barrier(jnp.sum(basis_one * image_one, axis=(1, 2)))
    remainder = image_one - alpha_one[:, None, None] * basis_one
    beta_one = jnp.sqrt(lax.optimization_barrier(jnp.sum(remainder * remainder, axis=(1, 2))) + 1e-06)
    basis_two = remainder / beta_one[:, None, None]
    image_two = apply_mobility(positions, basis_two)
    alpha_two = lax.optimization_barrier(jnp.sum(basis_two * image_two, axis=(1, 2)))
    det_root = jnp.sqrt(alpha_one * alpha_two - beta_one * beta_one)
    trace_root = jnp.sqrt(alpha_one + alpha_two + 2.0 * det_root)
    weight_one = (alpha_one + det_root) / trace_root
    weight_two = beta_one / trace_root
    return 0.5 * noise_length[:, None, None] * (weight_one[:, None, None] * basis_one + weight_two[:, None, None] * basis_two)
```

```python
import functools

import jax
import jax.numpy as jnp
from jax import lax
from jax.experimental import pallas as pl
from jax.experimental.pallas import tpu as pltpu
from jax.sharding import PartitionSpec as P

LANES = 128
MESH = pl.DeviceIdType.MESH
BLOCKS = ((0, 0), (1, 1), (2, 2), (0, 1), (0, 2), (1, 2))


def replicated_kernel(
    rows,
    cols,
    noise_ref,
    pos_ref,
    out_ref,
    gathered,
    stage,
    own_ref,
    noise_full,
    pos_cols,
    pos_rows,
    mobility,
    weights,
    image,
    send_col,
    recv_col,
    send_row,
    recv_row,
):
    _, per_device, samples = noise_ref.shape
    particles = rows * cols * per_device
    f32, bf16 = jnp.float32, jnp.bfloat16
    my_row, my_col = lax.axis_index("row"), lax.axis_index("col")

    col_peers = [lax.rem(my_col + k, cols) for k in range(1, cols)]
    row_peers = [lax.rem(my_row + k, rows) for k in range(1, rows)]

    barrier = pltpu.get_barrier_semaphore()
    for peer in col_peers:
        pl.semaphore_signal(barrier, inc=1, device_id=(my_row, peer), device_id_type=MESH)
    for peer in row_peers:
        pl.semaphore_signal(barrier, inc=1, device_id=(peer, my_col), device_id_type=MESH)

    stage[...] = jnp.zeros_like(stage)
    position = pos_ref[...]
    for term in range(3):
        piece = position.astype(bf16).astype(f32)
        stage[pl.ds(3 * term, 3), pl.ds(0, per_device)] = piece
        position = position - piece
    turned = jnp.transpose(stage[...])
    own_ref[...] = jnp.zeros_like(own_ref)
    for b in range(3):
        own_ref[:, pl.ds(b * samples, samples)] = noise_ref[b]
    own_ref[:, pl.ds(3 * samples, 16)] = turned[0:per_device, :]
    own = own_ref[...]
    gathered[my_row, my_col] = own.astype(bf16)

    pl.semaphore_wait(barrier, cols + rows - 2)

    def col_copy(peer, source):
        return pltpu.make_async_remote_copy(
            src_ref=gathered.at[my_row, my_col],
            dst_ref=gathered.at[my_row, my_col],
            send_sem=send_col.at[peer],
            recv_sem=recv_col.at[source],
            device_id=(my_row, peer),
            device_id_type=MESH,
        )

    def row_copy(block, peer):
        return pltpu.make_async_remote_copy(
            src_ref=gathered.at[my_row, block],
            dst_ref=gathered.at[my_row, block],
            send_sem=send_row.at[peer],
            recv_sem=recv_row.at[my_row],
            device_id=(peer, my_col),
            device_id_type=MESH,
        )

    for peer in col_peers:
        col_copy(peer, my_col).start()
    for peer in row_peers:
        row_copy(my_col, peer).start()
    for k in range(1, cols):
        source = lax.rem(my_col + cols - k, cols)
        pltpu.make_async_copy(
            gathered.at[my_row, source], gathered.at[my_row, source], recv_col.at[source]
        ).wait()
        for peer in row_peers:
            row_copy(source, peer).start()
    for peer in row_peers:
        pltpu.make_async_copy(gathered.at[peer], gathered.at[peer], recv_row.at[peer]).wait()

    packed = gathered[...].reshape(particles, LANES)
    lane = lax.broadcasted_iota(jnp.int32, (1, LANES), 1)
    field = lax.broadcasted_iota(jnp.int32, (LANES, 3 * LANES), 0) - 3 * samples
    target = lax.broadcasted_iota(jnp.int32, (LANES, 3 * LANES), 1) // LANES
    select = (field == target) | (field == target + 3) | (field == target + 6)
    pos_cols[...] = jnp.dot(packed, select.astype(f32).astype(bf16), preferred_element_type=f32)
    field = lax.broadcasted_iota(jnp.int32, (3 * 16, LANES), 1) - 3 * samples
    target = lax.broadcasted_iota(jnp.int32, (3 * 16, LANES), 0) // 16
    select = (field == target) | (field == target + 3) | (field == target + 6)
    pos_rows[...] = lax.dot_general(
        select.astype(f32).astype(bf16), packed, (((1,), (1,)), ((), ())), preferred_element_type=f32
    )

    @pl.loop(0, particles // 16)
    def _(step):
        start = pl.multiple_of(step * 16, 16)
        at_rows = pl.ds(start, 16)
        row_pos = [pos_cols[at_rows, pl.ds(a * LANES, LANES)] for a in range(3)]
        row_label = start + lax.broadcasted_iota(jnp.int32, (16, LANES), 0)
        for tile in range(particles // LANES):
            at_cols = pl.ds(tile * LANES, LANES)
            d = [row_pos[a] - pos_rows[pl.ds(a * 16, 16), at_cols] for a in range(3)]
            col_label = tile * LANES + lax.broadcasted_iota(jnp.int32, (16, LANES), 1)
            retain = row_label != col_label
            q = jnp.where(retain, d[0] * d[0] + d[1] * d[1] + d[2] * d[2], 4.0)
            u = lax.rsqrt(q)
            r = q * u
            near = r < 2.0
            u2 = u * u
            f = jnp.where(near, 1.0 - 0.28125 * r, u * (0.75 + 0.5 * u2))
            f = jnp.where(retain, f, 0.0)
            h = u * jnp.where(near, 0.09375, u2 * (0.75 - 1.5 * u2))
            hd = [h * d[a] for a in range(3)]
            for n, (a, b) in enumerate(BLOCKS):
                element = hd[a] * d[b]
                if a == b:
                    element = element + f
                mobility[at_rows, pl.ds(n * particles + tile * LANES, LANES)] = element.astype(bf16)

    def set_weights(x):
        down = pltpu.roll(x, LANES - samples, 1)
        up = pltpu.roll(x, samples, 1)
        across = pltpu.roll(x, 2 * samples, 1)
        group = lane // samples
        moved = {
            (0, 0): jnp.where(group == 0, x, 0.0),
            (1, 1): jnp.where(group == 1, x, 0.0),
            (2, 2): jnp.where(group == 2, x, 0.0),
            (0, 1): jnp.where(group == 0, down, jnp.where(group == 1, up, 0.0)),
            (1, 2): jnp.where(group == 1, down, jnp.where(group == 2, up, 0.0)),
            (0, 2): jnp.where((group == 0) | (group == 2), across, 0.0),
        }
        for n, pair in enumerate(BLOCKS):
            weights[pl.ds(n * particles, particles), :] = moved[pair].astype(bf16)

    def total(x):
        column = jnp.sum(x, axis=0, keepdims=True)
        column = jnp.broadcast_to(column, (8, LANES))
        column = column + pltpu.roll(column, 2 * samples, 1)
        column = column + pltpu.roll(column, samples, 1)
        return column[0:1, :]

    is_noise = lane < 3 * samples
    me = pl.multiple_of((my_row * cols + my_col) * per_device, per_device)
    at_own = pl.ds(me, per_device)
    wide = packed.astype(f32)
    set_weights(wide)
    noise_full[...] = jnp.where(is_noise, wide, 0.0)
    noise_full[at_own, :] = jnp.where(is_noise, own_ref[...], 0.0)

    noise = noise_full[...]
    length = jnp.sqrt(total(noise * noise) + 1e-06)
    inverse = 1.0 / length
    coupled = jnp.dot(mobility[...], weights[...], preferred_element_type=f32)
    basis_one = noise * inverse
    image_one = basis_one + coupled * inverse
    alpha_one = total(basis_one * image_one)
    remainder = image_one - alpha_one * basis_one
    beta_one = jnp.sqrt(total(remainder * remainder) + 1e-06)
    basis_two = remainder * (1.0 / beta_one)
    image[...] = basis_two
    set_weights(basis_two)
    coupled = jnp.dot(mobility[...], weights[...], preferred_element_type=f32)
    basis_two = image[...]
    alpha_two = total(basis_two * (basis_two + coupled))
    det_root = jnp.sqrt(alpha_one * alpha_two - beta_one * beta_one)
    trace_root = jnp.sqrt(alpha_one + alpha_two + 2.0 * det_root)
    weight_one = (alpha_one + det_root) / trace_root
    weight_two = beta_one / trace_root
    own_one = noise_full[at_own, :] * inverse
    own_two = image[at_own, :]
    result = 0.5 * length * (weight_one * own_one + weight_two * own_two)
    for b in range(3):
        out_ref[b] = result[:, b * samples : (b + 1) * samples]

    for peer in col_peers:
        col_copy(peer, my_col).wait_send()
    for peer in row_peers:
        pltpu.make_async_copy(gathered.at[my_row], gathered.at[my_row], send_row.at[peer]).wait()


def replicated(mesh, positions, thermal_noise):
    rows, cols = mesh.shape["row"], mesh.shape["col"]
    samples, _, per_device = thermal_noise.shape
    particles = rows * cols * per_device
    f32, bf16 = jnp.float32, jnp.bfloat16
    vmem = pl.BlockSpec(memory_space=pltpu.VMEM)
    out = pl.pallas_call(
        functools.partial(replicated_kernel, rows, cols),
        out_shape=jax.ShapeDtypeStruct((3, per_device, samples), f32),
        in_specs=[vmem, vmem],
        out_specs=vmem,
        scratch_shapes=[
            pltpu.VMEM((rows, cols, per_device, LANES), bf16),
            pltpu.VMEM((16, LANES), f32),
            pltpu.VMEM((per_device, LANES), f32),
            pltpu.VMEM((particles, LANES), f32),
            pltpu.VMEM((particles, 3 * LANES), f32),
            pltpu.VMEM((3 * 16, particles), f32),
            pltpu.VMEM((particles, 6 * particles), bf16),
            pltpu.VMEM((6 * particles, LANES), bf16),
            pltpu.VMEM((particles, LANES), f32),
            pltpu.SemaphoreType.DMA((cols,)),
            pltpu.SemaphoreType.DMA((cols,)),
            pltpu.SemaphoreType.DMA((rows,)),
            pltpu.SemaphoreType.DMA((rows,)),
        ],
        compiler_params=pltpu.CompilerParams(collective_id=0, has_side_effects=True),
        name="lanczos",
    )(jnp.transpose(thermal_noise, (1, 2, 0)), positions)
    return jnp.transpose(out, (2, 0, 1))


def fits(mesh, positions, thermal_noise):
    devices = mesh.shape["row"] * mesh.shape["col"]
    samples, _, particles = thermal_noise.shape
    per_device = particles // devices
    return (
        4 * samples == LANES
        and per_device % 16 == 0
        and particles % LANES == 0
        and 12 * particles * particles <= 2**24
    )


def pair_tensor(rows_pos, cols_pos, retain):
    offsets = [rows_pos[a][None, :] - cols_pos[a][:, None] for a in range(3)]
    squared = offsets[0] * offsets[0] + offsets[1] * offsets[1] + offsets[2] * offsets[2]
    guarded = jnp.where(retain, squared, 4.0)
    inverse = lax.rsqrt(guarded)
    distance = guarded * inverse
    correlation = distance < 2.0
    inverse_cube = inverse * inverse * inverse
    inverse_fifth = inverse_cube * inverse * inverse
    isotropic = jnp.where(
        correlation, 1.0 - 0.28125 * distance, 0.75 * inverse + 0.5 * inverse_cube
    )
    dyadic = jnp.where(correlation, 0.09375 * inverse, 0.75 * inverse_cube - 1.5 * inverse_fifth)
    isotropic = jnp.where(retain, isotropic, 0.0)
    dyadic = jnp.where(retain, dyadic, 0.0)
    columns = []
    for b in range(3):
        elements = []
        for a in range(3):
            element = dyadic * offsets[a] * offsets[b]
            if a == b:
                element = element + isotropic
            elements.append(element)
        columns.append(jnp.stack(elements, axis=1))
    return jnp.stack(columns, axis=0)


def half_image(pos_rows, pos_cols, vec_rows, vec_cols, own_vector):
    row_devices = lax.axis_size("row")
    col_devices = lax.axis_size("col")
    row_index = lax.axis_index("row")
    col_index = lax.axis_index("col")
    samples = own_vector.shape[0]
    per_device = own_vector.shape[2]
    row_count = pos_rows.shape[1]
    row_label = row_index * col_devices * per_device + lax.iota(jnp.int32, row_count)
    group_size = min(row_devices, max(1, 128 // per_device))
    width = group_size * per_device
    group_count = row_devices // group_size
    sum_rows = jnp.zeros((samples, 3, row_count), jnp.float32)
    sum_cols = jnp.zeros((samples, 3, per_device * row_devices), jnp.float32)

    def add_group(group, totals):
        sum_rows, sum_cols = totals
        start = group * width
        cols_pos = lax.dynamic_slice_in_dim(pos_cols, start, width, 1)
        cols_vec = lax.dynamic_slice_in_dim(vec_cols, start, width, 2)
        local_cols = lax.iota(jnp.int32, width)
        segment = group * group_size + local_cols // per_device
        col_label = (segment * col_devices + col_index) * per_device + local_cols % per_device
        keep = segment >= row_index
        upper = (segment != row_index)[:, None] | (row_label[None, :] < col_label[:, None])
        retain = keep[:, None] & upper & (row_label[None, :] != col_label[:, None])
        tensor = pair_tensor(pos_rows, cols_pos, retain).astype(jnp.bfloat16)
        sum_rows = sum_rows + jnp.einsum(
            "kbj,bjai->kai", cols_vec, tensor, preferred_element_type=jnp.float32
        )
        credit = jnp.einsum("kai,bjai->kbj", vec_rows, tensor, preferred_element_type=jnp.float32)
        previous = lax.dynamic_slice_in_dim(sum_cols, start, width, 2)
        sum_cols = lax.dynamic_update_slice_in_dim(sum_cols, previous + credit, start, 2)
        return (sum_rows, sum_cols)

    totals = (sum_rows, sum_cols)
    totals = lax.fori_loop(row_index // group_size, group_count, add_group, totals)
    sum_rows, sum_cols = totals
    mobility_image = own_vector + lax.psum_scatter(sum_rows, "col", scatter_dimension=2, tiled=True)
    return mobility_image + lax.psum_scatter(sum_cols, "row", scatter_dimension=2, tiled=True)


def on_device(positions, thermal_noise):
    squares = lax.psum(jnp.sum(thermal_noise * thermal_noise, axis=(1, 2)), ("row", "col"))
    noise_length = jnp.sqrt(squares + 1e-06)
    basis_one = thermal_noise / noise_length[:, None, None]
    pos_cols, cols_one = (
        lax.all_gather(positions, "row", axis=1, tiled=True),
        lax.all_gather(basis_one, "row", axis=2, tiled=True),
    )
    pos_rows, rows_wide = (
        lax.all_gather(positions, "col", axis=1, tiled=True),
        lax.all_gather(basis_one, "col", axis=2, tiled=True),
    )
    image_one = half_image(
        pos_rows, pos_cols, rows_wide.astype(jnp.bfloat16), cols_one.astype(jnp.bfloat16), basis_one
    )
    alpha_one = lax.psum(jnp.sum(basis_one * image_one, axis=(1, 2)), ("row", "col"))
    remainder = image_one - alpha_one[:, None, None] * basis_one
    beta_squared = lax.psum(jnp.sum(remainder * remainder, axis=(1, 2)), ("row", "col"))
    beta_one = jnp.sqrt(beta_squared + 1e-06)
    basis_two = remainder / beta_one[:, None, None]
    narrow_two = basis_two.astype(jnp.bfloat16)
    cols_two = lax.all_gather(narrow_two, "row", axis=2, tiled=True)
    rows_two = lax.all_gather(narrow_two, "col", axis=2, tiled=True)
    image_two = half_image(pos_rows, pos_cols, rows_two, cols_two, basis_two)
    alpha_two = lax.psum(jnp.sum(basis_two * image_two, axis=(1, 2)), ("row", "col"))
    det_root = jnp.sqrt(alpha_one * alpha_two - beta_one * beta_one)
    trace_root = jnp.sqrt(alpha_one + alpha_two + 2.0 * det_root)
    weight_one = (alpha_one + det_root) / trace_root
    weight_two = beta_one / trace_root
    return (
        0.5
        * noise_length[:, None, None]
        * (weight_one[:, None, None] * basis_one + weight_two[:, None, None] * basis_two)
    )


def solution(mesh):
    specs = dict(
        mesh=mesh,
        in_specs=(P(None, ("row", "col")), P(None, None, ("row", "col"))),
        out_specs=P(None, None, ("row", "col")),
        check_vma=False,
    )

    def program(positions, thermal_noise):
        if fits(mesh, positions, thermal_noise):
            body = functools.partial(replicated, mesh)
        else:
            body = on_device
        return jax.shard_map(body, **specs)(positions, thermal_noise)

    return program
```

```python
import functools

import jax
import jax.numpy as jnp
from jax import lax
from jax.experimental import pallas as pl
from jax.experimental.pallas import tpu as pltpu
from jax.sharding import PartitionSpec as P

LANES = 128
MESH = pl.DeviceIdType.MESH
BLOCKS = ((0, 0), (1, 1), (2, 2), (0, 1), (0, 2), (1, 2))


def partner(place, k, size):
    if size & (size - 1):
        return lax.rem(place + k, size)
    result = 0
    bit = 1
    while bit < size:
        digit = lax.rem(place // bit, 2)
        result = result + bit * (1 - digit if k & bit else digit)
        bit = 2 * bit
    return result


def replicated_kernel(
    rows,
    outer,
    inner,
    noise_ref,
    pos_ref,
    out_ref,
    gathered,
    stage,
    own_ref,
    noise_full,
    pos_cols,
    pos_rows,
    mobility,
    weights,
    image,
    send_line,
    recv_line,
    send_plane,
    recv_plane,
):
    _, per_device, samples = noise_ref.shape
    particles = rows * outer * inner * per_device
    f32, bf16 = jnp.float32, jnp.bfloat16
    my_row, my_col = lax.axis_index("row"), lax.axis_index("col")

    my_outer, my_inner = my_col // inner, lax.rem(my_col, inner)
    line = [partner(my_outer, k, outer) for k in range(1, outer)]
    plane = [
        (partner(my_row, j, rows), partner(my_inner, i, inner))
        for i in range(inner)
        for j in range(rows)
        if i or j
    ]

    barrier = pltpu.get_barrier_semaphore()
    for place in line:
        pl.semaphore_signal(
            barrier, inc=1, device_id=(my_row, place * inner + my_inner), device_id_type=MESH
        )
    for row, place in plane:
        pl.semaphore_signal(
            barrier, inc=1, device_id=(row, my_outer * inner + place), device_id_type=MESH
        )

    stage[...] = jnp.zeros_like(stage)
    position = pos_ref[...]
    for term in range(3):
        piece = position.astype(bf16).astype(f32)
        stage[pl.ds(3 * term, 3), pl.ds(0, per_device)] = piece
        position = position - piece
    turned = jnp.transpose(stage[...])
    own_ref[...] = jnp.zeros_like(own_ref)
    for b in range(3):
        own_ref[:, pl.ds(b * samples, samples)] = noise_ref[b]
    own_ref[:, pl.ds(3 * samples, 16)] = turned[0:per_device, :]
    own = own_ref[...]
    gathered[my_row, my_inner, my_outer] = own.astype(bf16)

    pl.semaphore_wait(barrier, len(line) + len(plane))

    def line_copy(place, source):
        return pltpu.make_async_remote_copy(
            src_ref=gathered.at[my_row, my_inner, my_outer],
            dst_ref=gathered.at[my_row, my_inner, my_outer],
            send_sem=send_line.at[place],
            recv_sem=recv_line.at[source],
            device_id=(my_row, place * inner + my_inner),
            device_id_type=MESH,
        )

    def plane_copy(block, row, place):
        return pltpu.make_async_remote_copy(
            src_ref=gathered.at[my_row, my_inner, block],
            dst_ref=gathered.at[my_row, my_inner, block],
            send_sem=send_plane.at[row, place],
            recv_sem=recv_plane.at[my_row, my_inner],
            device_id=(row, my_outer * inner + place),
            device_id_type=MESH,
        )

    def arrived(ref, semaphore):
        pltpu.make_async_copy(ref, ref, semaphore).wait()

    for place in line[::-1]:
        line_copy(place, my_outer).start()
    for row, place in plane:
        plane_copy(my_outer, row, place).start()
    for source in line:
        arrived(gathered.at[my_row, my_inner, source], recv_line.at[source])
        for row, place in plane:
            plane_copy(source, row, place).start()
    for row, place in plane:
        arrived(gathered.at[row, place], recv_plane.at[row, place])

    packed = gathered[...].reshape(particles, LANES)
    lane = lax.broadcasted_iota(jnp.int32, (1, LANES), 1)
    field = lax.broadcasted_iota(jnp.int32, (LANES, 3 * LANES), 0) - 3 * samples
    target = lax.broadcasted_iota(jnp.int32, (LANES, 3 * LANES), 1) // LANES
    select = (field == target) | (field == target + 3) | (field == target + 6)
    pos_cols[...] = jnp.dot(packed, select.astype(f32).astype(bf16), preferred_element_type=f32)
    field = lax.broadcasted_iota(jnp.int32, (3 * 16, LANES), 1) - 3 * samples
    target = lax.broadcasted_iota(jnp.int32, (3 * 16, LANES), 0) // 16
    select = (field == target) | (field == target + 3) | (field == target + 6)
    pos_rows[...] = lax.dot_general(
        select.astype(f32).astype(bf16), packed, (((1,), (1,)), ((), ())), preferred_element_type=f32
    )

    tiles = particles // LANES

    @pl.loop(0, particles // 16)
    def _(step):
        start = pl.multiple_of(step * 16, 16)
        at_rows = pl.ds(start, 16)
        row_pos = [pos_cols[at_rows, pl.ds(a * LANES, LANES)] for a in range(3)]
        row_label = start + lax.broadcasted_iota(jnp.int32, (16, LANES), 0)
        for tile in range(tiles):
            at_cols = pl.ds(tile * LANES, LANES)
            d = [row_pos[a] - pos_rows[pl.ds(a * 16, 16), at_cols] for a in range(3)]
            col_label = tile * LANES + lax.broadcasted_iota(jnp.int32, (16, LANES), 1)
            retain = row_label != col_label
            q = jnp.where(retain, d[0] * d[0] + d[1] * d[1] + d[2] * d[2], 4.0)
            u = lax.rsqrt(q)
            r = q * u
            near = r < 2.0
            u2 = u * u
            f = jnp.where(near, 1.0 - 0.28125 * r, u * (0.75 + 0.5 * u2))
            f = jnp.where(retain, f, 0.0)
            h = u * jnp.where(near, 0.09375, u2 * (0.75 - 1.5 * u2))
            hd = [h * d[a] for a in range(3)]
            for n, (a, b) in enumerate(BLOCKS):
                element = hd[a] * d[b]
                if a == b:
                    element = element + f
                mobility[n * tiles + tile, at_rows, :] = element.astype(bf16)

    def set_weights(x):
        down = pltpu.roll(x, LANES - samples, 1)
        up = pltpu.roll(x, samples, 1)
        across = pltpu.roll(x, 2 * samples, 1)
        group = lane // samples
        moved = {
            (0, 0): jnp.where(group == 0, x, 0.0),
            (1, 1): jnp.where(group == 1, x, 0.0),
            (2, 2): jnp.where(group == 2, x, 0.0),
            (0, 1): jnp.where(group == 0, down, jnp.where(group == 1, up, 0.0)),
            (1, 2): jnp.where(group == 1, down, jnp.where(group == 2, up, 0.0)),
            (0, 2): jnp.where((group == 0) | (group == 2), across, 0.0),
        }
        for n, pair in enumerate(BLOCKS):
            weights[pl.ds(n * particles, particles), :] = moved[pair].astype(bf16)

    def total(x):
        column = jnp.sum(x, axis=0, keepdims=True)
        column = jnp.broadcast_to(column, (8, LANES))
        column = column + pltpu.roll(column, 2 * samples, 1)
        column = column + pltpu.roll(column, samples, 1)
        return column[0:1, :]

    def couple():
        half = particles // 2
        parts = []
        for start in (0, half):
            chunk = jnp.concatenate(
                [mobility[slab, pl.ds(start, half), :] for slab in range(6 * tiles)], axis=1
            )
            parts.append(jnp.dot(chunk, weights[...], preferred_element_type=f32))
        return jnp.concatenate(parts, axis=0)

    is_noise = lane < 3 * samples
    me = pl.multiple_of(((my_row * inner + my_inner) * outer + my_outer) * per_device, per_device)
    at_own = pl.ds(me, per_device)
    wide = packed.astype(f32)
    set_weights(wide)
    noise_full[...] = jnp.where(is_noise, wide, 0.0)
    noise_full[at_own, :] = jnp.where(is_noise, own_ref[...], 0.0)

    noise = noise_full[...]
    length = jnp.sqrt(total(noise * noise) + 1e-06)
    inverse = 1.0 / length
    coupled = couple()
    basis_one = noise * inverse
    image_one = basis_one + coupled * inverse
    alpha_one = total(basis_one * image_one)
    remainder = image_one - alpha_one * basis_one
    beta_one = jnp.sqrt(total(remainder * remainder) + 1e-06)
    basis_two = remainder * (1.0 / beta_one)
    image[...] = basis_two
    set_weights(basis_two)
    coupled = couple()
    basis_two = image[...]
    alpha_two = total(basis_two * (basis_two + coupled))
    det_root = jnp.sqrt(alpha_one * alpha_two - beta_one * beta_one)
    trace_root = jnp.sqrt(alpha_one + alpha_two + 2.0 * det_root)
    weight_one = (alpha_one + det_root) / trace_root
    weight_two = beta_one / trace_root
    own_one = noise_full[at_own, :] * inverse
    own_two = image[at_own, :]
    result = 0.5 * length * (weight_one * own_one + weight_two * own_two)
    for b in range(3):
        out_ref[b] = result[:, b * samples : (b + 1) * samples]

    for place in line:
        line_copy(place, my_outer).wait_send()
    for row, place in plane:
        arrived(gathered.at[my_row, my_inner], send_plane.at[row, place])


def replicated(mesh, positions, thermal_noise):
    rows, cols = mesh.shape["row"], mesh.shape["col"]
    samples, _, per_device = thermal_noise.shape
    particles = rows * cols * per_device
    inner = 2 if cols % 2 == 0 else 1
    outer = cols // inner
    f32, bf16 = jnp.float32, jnp.bfloat16
    vmem = pl.BlockSpec(memory_space=pltpu.VMEM)
    out = pl.pallas_call(
        functools.partial(replicated_kernel, rows, outer, inner),
        out_shape=jax.ShapeDtypeStruct((3, per_device, samples), f32),
        in_specs=[vmem, vmem],
        out_specs=vmem,
        scratch_shapes=[
            pltpu.VMEM((rows, inner, outer, per_device, LANES), bf16),
            pltpu.VMEM((16, LANES), f32),
            pltpu.VMEM((per_device, LANES), f32),
            pltpu.VMEM((particles, LANES), f32),
            pltpu.VMEM((particles, 3 * LANES), f32),
            pltpu.VMEM((3 * 16, particles), f32),
            pltpu.VMEM((6 * particles // LANES, particles, LANES), bf16),
            pltpu.VMEM((6 * particles, LANES), bf16),
            pltpu.VMEM((particles, LANES), f32),
            pltpu.SemaphoreType.DMA((outer,)),
            pltpu.SemaphoreType.DMA((outer,)),
            pltpu.SemaphoreType.DMA((rows, inner)),
            pltpu.SemaphoreType.DMA((rows, inner)),
        ],
        compiler_params=pltpu.CompilerParams(collective_id=0, has_side_effects=True),
        name="lanczos",
    )(jnp.transpose(thermal_noise, (1, 2, 0)), positions)
    return jnp.transpose(out, (2, 0, 1))


def fits(mesh, positions, thermal_noise):
    devices = mesh.shape["row"] * mesh.shape["col"]
    samples, _, particles = thermal_noise.shape
    per_device = particles // devices
    return (
        4 * samples == LANES
        and per_device % 16 == 0
        and particles % LANES == 0
        and 12 * particles * particles <= 2**24
    )


def pair_tensor(rows_pos, cols_pos, retain):
    offsets = [rows_pos[a][None, :] - cols_pos[a][:, None] for a in range(3)]
    squared = offsets[0] * offsets[0] + offsets[1] * offsets[1] + offsets[2] * offsets[2]
    guarded = jnp.where(retain, squared, 4.0)
    inverse = lax.rsqrt(guarded)
    distance = guarded * inverse
    correlation = distance < 2.0
    inverse_cube = inverse * inverse * inverse
    inverse_fifth = inverse_cube * inverse * inverse
    isotropic = jnp.where(
        correlation, 1.0 - 0.28125 * distance, 0.75 * inverse + 0.5 * inverse_cube
    )
    dyadic = jnp.where(correlation, 0.09375 * inverse, 0.75 * inverse_cube - 1.5 * inverse_fifth)
    isotropic = jnp.where(retain, isotropic, 0.0)
    dyadic = jnp.where(retain, dyadic, 0.0)
    columns = []
    for b in range(3):
        elements = []
        for a in range(3):
            element = dyadic * offsets[a] * offsets[b]
            if a == b:
                element = element + isotropic
            elements.append(element)
        columns.append(jnp.stack(elements, axis=1))
    return jnp.stack(columns, axis=0)


def half_image(pos_rows, pos_cols, vec_rows, vec_cols, own_vector):
    row_devices = lax.axis_size("row")
    col_devices = lax.axis_size("col")
    row_index = lax.axis_index("row")
    col_index = lax.axis_index("col")
    samples = own_vector.shape[0]
    per_device = own_vector.shape[2]
    row_count = pos_rows.shape[1]
    row_label = row_index * col_devices * per_device + lax.iota(jnp.int32, row_count)
    group_size = min(row_devices, max(1, 128 // per_device))
    width = group_size * per_device
    group_count = row_devices // group_size
    sum_rows = jnp.zeros((samples, 3, row_count), jnp.float32)
    sum_cols = jnp.zeros((samples, 3, per_device * row_devices), jnp.float32)

    def add_group(group, totals):
        sum_rows, sum_cols = totals
        start = group * width
        cols_pos = lax.dynamic_slice_in_dim(pos_cols, start, width, 1)
        cols_vec = lax.dynamic_slice_in_dim(vec_cols, start, width, 2)
        local_cols = lax.iota(jnp.int32, width)
        segment = group * group_size + local_cols // per_device
        col_label = (segment * col_devices + col_index) * per_device + local_cols % per_device
        keep = segment >= row_index
        upper = (segment != row_index)[:, None] | (row_label[None, :] < col_label[:, None])
        retain = keep[:, None] & upper & (row_label[None, :] != col_label[:, None])
        tensor = pair_tensor(pos_rows, cols_pos, retain).astype(jnp.bfloat16)
        sum_rows = sum_rows + jnp.einsum(
            "kbj,bjai->kai", cols_vec, tensor, preferred_element_type=jnp.float32
        )
        credit = jnp.einsum("kai,bjai->kbj", vec_rows, tensor, preferred_element_type=jnp.float32)
        previous = lax.dynamic_slice_in_dim(sum_cols, start, width, 2)
        sum_cols = lax.dynamic_update_slice_in_dim(sum_cols, previous + credit, start, 2)
        return (sum_rows, sum_cols)

    totals = (sum_rows, sum_cols)
    totals = lax.fori_loop(row_index // group_size, group_count, add_group, totals)
    sum_rows, sum_cols = totals
    mobility_image = own_vector + lax.psum_scatter(sum_rows, "col", scatter_dimension=2, tiled=True)
    return mobility_image + lax.psum_scatter(sum_cols, "row", scatter_dimension=2, tiled=True)


def on_device(positions, thermal_noise):
    squares = lax.psum(jnp.sum(thermal_noise * thermal_noise, axis=(1, 2)), ("row", "col"))
    noise_length = jnp.sqrt(squares + 1e-06)
    basis_one = thermal_noise / noise_length[:, None, None]
    pos_cols, cols_one = (
        lax.all_gather(positions, "row", axis=1, tiled=True),
        lax.all_gather(basis_one, "row", axis=2, tiled=True),
    )
    pos_rows, rows_wide = (
        lax.all_gather(positions, "col", axis=1, tiled=True),
        lax.all_gather(basis_one, "col", axis=2, tiled=True),
    )
    image_one = half_image(
        pos_rows, pos_cols, rows_wide.astype(jnp.bfloat16), cols_one.astype(jnp.bfloat16), basis_one
    )
    alpha_one = lax.psum(jnp.sum(basis_one * image_one, axis=(1, 2)), ("row", "col"))
    remainder = image_one - alpha_one[:, None, None] * basis_one
    beta_squared = lax.psum(jnp.sum(remainder * remainder, axis=(1, 2)), ("row", "col"))
    beta_one = jnp.sqrt(beta_squared + 1e-06)
    basis_two = remainder / beta_one[:, None, None]
    narrow_two = basis_two.astype(jnp.bfloat16)
    cols_two = lax.all_gather(narrow_two, "row", axis=2, tiled=True)
    rows_two = lax.all_gather(narrow_two, "col", axis=2, tiled=True)
    image_two = half_image(pos_rows, pos_cols, rows_two, cols_two, basis_two)
    alpha_two = lax.psum(jnp.sum(basis_two * image_two, axis=(1, 2)), ("row", "col"))
    det_root = jnp.sqrt(alpha_one * alpha_two - beta_one * beta_one)
    trace_root = jnp.sqrt(alpha_one + alpha_two + 2.0 * det_root)
    weight_one = (alpha_one + det_root) / trace_root
    weight_two = beta_one / trace_root
    return (
        0.5
        * noise_length[:, None, None]
        * (weight_one[:, None, None] * basis_one + weight_two[:, None, None] * basis_two)
    )


def solution(mesh):
    specs = dict(
        mesh=mesh,
        in_specs=(P(None, ("row", "col")), P(None, None, ("row", "col"))),
        out_specs=P(None, None, ("row", "col")),
        check_vma=False,
    )

    def program(positions, thermal_noise):
        if fits(mesh, positions, thermal_noise):
            body = functools.partial(replicated, mesh)
        else:
            body = on_device
        return jax.shard_map(body, **specs)(positions, thermal_noise)

    return program
```

```python
import functools

import jax
import jax.numpy as jnp
from jax import lax
from jax.experimental import pallas as pl
from jax.experimental.pallas import tpu as pltpu
from jax.sharding import PartitionSpec as P

LANES = 128
MESH = pl.DeviceIdType.MESH
BLOCKS = ((0, 0), (1, 1), (2, 2), (0, 1), (0, 2), (1, 2))


def partner(place, k, size):
    result = 0
    bit = 1
    while bit < size:
        digit = lax.rem(place // bit, 2)
        result = result + bit * (1 - digit if k & bit else digit)
        bit = 2 * bit
    return result


def replicated_kernel(
    rows,
    outer,
    inner,
    noise_ref,
    pos_ref,
    out_ref,
    gathered,
    stage,
    own_ref,
    noise_full,
    pos_cols,
    pos_rows,
    mobility,
    weights,
    image,
    send_line,
    recv_line,
    send_plane,
    recv_plane,
):
    _, per_device, samples = noise_ref.shape
    particles = rows * outer * inner * per_device
    f32, bf16 = jnp.float32, jnp.bfloat16
    my_row, my_col = lax.axis_index("row"), lax.axis_index("col")

    my_outer, my_inner = my_col // inner, lax.rem(my_col, inner)
    line = [partner(my_outer, k, outer) for k in range(outer)]
    plane = [
        (partner(my_row, j, rows), partner(my_inner, i, inner))
        for i in range(inner)
        for j in range(rows)
    ]

    barrier = pltpu.get_barrier_semaphore()
    for place in line[1:]:
        pl.semaphore_signal(
            barrier, inc=1, device_id=(my_row, place * inner + my_inner), device_id_type=MESH
        )
    for row, place in plane[1:]:
        pl.semaphore_signal(
            barrier, inc=1, device_id=(row, my_outer * inner + place), device_id_type=MESH
        )

    stage[...] = jnp.zeros_like(stage)
    position = pos_ref[...]
    for term in range(3):
        piece = position.astype(bf16).astype(f32)
        stage[pl.ds(3 * term, 3), pl.ds(0, per_device)] = piece
        position = position - piece
    turned = jnp.transpose(stage[...])
    own_ref[...] = jnp.zeros_like(own_ref)
    for b in range(3):
        own_ref[:, pl.ds(b * samples, samples)] = noise_ref[b]
    own_ref[:, pl.ds(3 * samples, 16)] = turned[0:per_device, :]
    own = own_ref[...]
    gathered[0, 0] = own.astype(bf16)

    pl.semaphore_wait(barrier, len(line) + len(plane) - 2)

    def line_copy(k):
        return pltpu.make_async_remote_copy(
            src_ref=gathered.at[0, 0],
            dst_ref=gathered.at[0, k],
            send_sem=send_line.at[k],
            recv_sem=recv_line.at[k],
            device_id=(my_row, line[k] * inner + my_inner),
            device_id_type=MESH,
        )

    def plane_copy(block, k):
        return pltpu.make_async_remote_copy(
            src_ref=gathered.at[0, block],
            dst_ref=gathered.at[k, block],
            send_sem=send_plane.at[k],
            recv_sem=recv_plane.at[k],
            device_id=(plane[k][0], my_outer * inner + plane[k][1]),
            device_id_type=MESH,
        )

    def finished(ref, semaphore):
        pltpu.make_async_copy(ref, ref, semaphore).wait()

    for k in range(outer - 1, 0, -1):
        line_copy(k).start()
    for k in range(1, len(plane)):
        plane_copy(0, k).start()
    for block in range(1, outer):
        finished(gathered.at[0, block], recv_line.at[block])
        for k in range(1, len(plane)):
            plane_copy(block, k).start()

    lane = lax.broadcasted_iota(jnp.int32, (1, LANES), 1)
    field = lax.broadcasted_iota(jnp.int32, (LANES, 3 * LANES), 0) - 3 * samples
    target = lax.broadcasted_iota(jnp.int32, (LANES, 3 * LANES), 1) // LANES
    select = (field == target) | (field == target + 3) | (field == target + 6)
    over_lanes = select.astype(f32).astype(bf16)
    field = lax.broadcasted_iota(jnp.int32, (3 * 16, LANES), 1) - 3 * samples
    target = lax.broadcasted_iota(jnp.int32, (3 * 16, LANES), 0) // 16
    select = (field == target) | (field == target + 3) | (field == target + 6)
    over_rows = select.astype(f32).astype(bf16)
    tiles = particles // LANES

    def form(start, tile, on_diagonal):
        at_rows = pl.ds(start, 16)
        d = [
            pos_cols[at_rows, pl.ds(a * LANES, LANES)]
            - pos_rows[pl.ds(a * 16, 16), pl.ds(tile * LANES, LANES)]
            for a in range(3)
        ]
        q = d[0] * d[0] + d[1] * d[1] + d[2] * d[2]
        if on_diagonal:
            row_label = start + lax.broadcasted_iota(jnp.int32, (16, LANES), 0)
            col_label = tile * LANES + lax.broadcasted_iota(jnp.int32, (16, LANES), 1)
            retain = row_label != col_label
            q = jnp.where(retain, q, 4.0)
        u = lax.rsqrt(q)
        r = q * u
        near = r < 2.0
        u2 = u * u
        f = jnp.where(near, 1.0 - 0.28125 * r, u * (0.75 + 0.5 * u2))
        if on_diagonal:
            f = jnp.where(retain, f, 0.0)
        h = u * jnp.where(near, 0.09375, u2 * (0.75 - 1.5 * u2))
        hd = [h * d[a] for a in range(3)]
        for n, (a, b) in enumerate(BLOCKS):
            element = hd[a] * d[b]
            if a == b:
                element = element + f
            mobility[n * tiles + tile, at_rows, :] = element.astype(bf16)

    per_tile = LANES // (outer * per_device)
    for tile in range(tiles):
        for k in range(tile * per_tile, (tile + 1) * per_tile):
            if k:
                finished(gathered.at[k], recv_plane.at[k])
        packed = gathered[pl.ds(tile * per_tile, per_tile)].reshape(LANES, LANES)
        pos_cols[pl.ds(tile * LANES, LANES), :] = jnp.dot(
            packed, over_lanes, preferred_element_type=f32
        )
        pos_rows[:, pl.ds(tile * LANES, LANES)] = lax.dot_general(
            over_rows, packed, (((1,), (1,)), ((), ())), preferred_element_type=f32
        )

        @pl.loop(0, LANES // 16)
        def _(step, tile=tile):
            for other in range(tile + 1):
                start = pl.multiple_of(tile * LANES + step * 16, 16)
                form(start, other, other == tile)
            for other in range(tile):
                start = pl.multiple_of(other * LANES + step * 16, 16)
                form(start, tile, False)

    packed = gathered[...].reshape(particles, LANES)

    def set_weights(x):
        down = pltpu.roll(x, LANES - samples, 1)
        up = pltpu.roll(x, samples, 1)
        across = pltpu.roll(x, 2 * samples, 1)
        group = lane // samples
        moved = {
            (0, 0): jnp.where(group == 0, x, 0.0),
            (1, 1): jnp.where(group == 1, x, 0.0),
            (2, 2): jnp.where(group == 2, x, 0.0),
            (0, 1): jnp.where(group == 0, down, jnp.where(group == 1, up, 0.0)),
            (1, 2): jnp.where(group == 1, down, jnp.where(group == 2, up, 0.0)),
            (0, 2): jnp.where((group == 0) | (group == 2), across, 0.0),
        }
        for n, pair in enumerate(BLOCKS):
            weights[pl.ds(n * particles, particles), :] = moved[pair].astype(bf16)

    def total(x):
        column = jnp.sum(x, axis=0, keepdims=True)
        column = jnp.broadcast_to(column, (8, LANES))
        column = column + pltpu.roll(column, 2 * samples, 1)
        column = column + pltpu.roll(column, samples, 1)
        return column[0:1, :]

    def couple():
        half = particles // 2
        parts = []
        for start in (0, half):
            chunk = jnp.concatenate(
                [mobility[slab, pl.ds(start, half), :] for slab in range(6 * tiles)], axis=1
            )
            parts.append(jnp.dot(chunk, weights[...], preferred_element_type=f32))
        return jnp.concatenate(parts, axis=0)

    is_noise = lane < 3 * samples
    at_own = pl.ds(0, per_device)
    wide = packed.astype(f32)
    set_weights(wide)
    noise_full[...] = jnp.where(is_noise, wide, 0.0)
    noise_full[at_own, :] = jnp.where(is_noise, own_ref[...], 0.0)

    noise = noise_full[...]
    length = jnp.sqrt(total(noise * noise) + 1e-06)
    inverse = 1.0 / length
    coupled = couple()
    basis_one = noise * inverse
    image_one = basis_one + coupled * inverse
    alpha_one = total(basis_one * image_one)
    remainder = image_one - alpha_one * basis_one
    beta_one = jnp.sqrt(total(remainder * remainder) + 1e-06)
    basis_two = remainder * (1.0 / beta_one)
    image[...] = basis_two
    set_weights(basis_two)
    coupled = couple()
    basis_two = image[...]
    alpha_two = total(basis_two * (basis_two + coupled))
    det_root = jnp.sqrt(alpha_one * alpha_two - beta_one * beta_one)
    trace_root = jnp.sqrt(alpha_one + alpha_two + 2.0 * det_root)
    weight_one = (alpha_one + det_root) / trace_root
    weight_two = beta_one / trace_root
    own_one = noise_full[at_own, :] * inverse
    own_two = image[at_own, :]
    result = 0.5 * length * (weight_one * own_one + weight_two * own_two)
    for b in range(3):
        out_ref[b] = result[:, b * samples : (b + 1) * samples]

    for k in range(1, outer):
        line_copy(k).wait_send()
    for k in range(1, len(plane)):
        finished(gathered.at[0], send_plane.at[k])


def replicated(mesh, positions, thermal_noise):
    rows, cols = mesh.shape["row"], mesh.shape["col"]
    samples, _, per_device = thermal_noise.shape
    particles = rows * cols * per_device
    inner = 2 if cols % 2 == 0 else 1
    outer = cols // inner
    f32, bf16 = jnp.float32, jnp.bfloat16
    vmem = pl.BlockSpec(memory_space=pltpu.VMEM)
    out = pl.pallas_call(
        functools.partial(replicated_kernel, rows, outer, inner),
        out_shape=jax.ShapeDtypeStruct((3, per_device, samples), f32),
        in_specs=[vmem, vmem],
        out_specs=vmem,
        scratch_shapes=[
            pltpu.VMEM((rows * inner, outer, per_device, LANES), bf16),
            pltpu.VMEM((16, LANES), f32),
            pltpu.VMEM((per_device, LANES), f32),
            pltpu.VMEM((particles, LANES), f32),
            pltpu.VMEM((particles, 3 * LANES), f32),
            pltpu.VMEM((3 * 16, particles), f32),
            pltpu.VMEM((6 * particles // LANES, particles, LANES), bf16),
            pltpu.VMEM((6 * particles, LANES), bf16),
            pltpu.VMEM((particles, LANES), f32),
            pltpu.SemaphoreType.DMA((outer,)),
            pltpu.SemaphoreType.DMA((outer,)),
            pltpu.SemaphoreType.DMA((rows * inner,)),
            pltpu.SemaphoreType.DMA((rows * inner,)),
        ],
        compiler_params=pltpu.CompilerParams(collective_id=0, has_side_effects=True),
        name="lanczos",
    )(jnp.transpose(thermal_noise, (1, 2, 0)), positions)
    return jnp.transpose(out, (2, 0, 1))


def fits(mesh, positions, thermal_noise):
    rows, cols = mesh.shape["row"], mesh.shape["col"]
    samples, _, particles = thermal_noise.shape
    per_device = particles // (rows * cols)
    outer = cols // 2 if cols % 2 == 0 else cols
    return (
        rows & (rows - 1) == 0
        and cols & (cols - 1) == 0
        and 4 * samples == LANES
        and per_device % 16 == 0
        and LANES % (outer * per_device) == 0
        and particles % (2 * LANES) == 0
        and 12 * particles * particles <= 2**24
    )


def pair_tensor(rows_pos, cols_pos, retain):
    offsets = [rows_pos[a][None, :] - cols_pos[a][:, None] for a in range(3)]
    squared = offsets[0] * offsets[0] + offsets[1] * offsets[1] + offsets[2] * offsets[2]
    guarded = jnp.where(retain, squared, 4.0)
    inverse = lax.rsqrt(guarded)
    distance = guarded * inverse
    correlation = distance < 2.0
    inverse_cube = inverse * inverse * inverse
    inverse_fifth = inverse_cube * inverse * inverse
    isotropic = jnp.where(
        correlation, 1.0 - 0.28125 * distance, 0.75 * inverse + 0.5 * inverse_cube
    )
    dyadic = jnp.where(correlation, 0.09375 * inverse, 0.75 * inverse_cube - 1.5 * inverse_fifth)
    isotropic = jnp.where(retain, isotropic, 0.0)
    dyadic = jnp.where(retain, dyadic, 0.0)
    columns = []
    for b in range(3):
        elements = []
        for a in range(3):
            element = dyadic * offsets[a] * offsets[b]
            if a == b:
                element = element + isotropic
            elements.append(element)
        columns.append(jnp.stack(elements, axis=1))
    return jnp.stack(columns, axis=0)


def half_image(pos_rows, pos_cols, vec_rows, vec_cols, own_vector):
    row_devices = lax.axis_size("row")
    col_devices = lax.axis_size("col")
    row_index = lax.axis_index("row")
    col_index = lax.axis_index("col")
    samples = own_vector.shape[0]
    per_device = own_vector.shape[2]
    row_count = pos_rows.shape[1]
    row_label = row_index * col_devices * per_device + lax.iota(jnp.int32, row_count)
    group_size = min(row_devices, max(1, 128 // per_device))
    width = group_size * per_device
    group_count = row_devices // group_size
    sum_rows = jnp.zeros((samples, 3, row_count), jnp.float32)
    sum_cols = jnp.zeros((samples, 3, per_device * row_devices), jnp.float32)

    def add_group(group, totals):
        sum_rows, sum_cols = totals
        start = group * width
        cols_pos = lax.dynamic_slice_in_dim(pos_cols, start, width, 1)
        cols_vec = lax.dynamic_slice_in_dim(vec_cols, start, width, 2)
        local_cols = lax.iota(jnp.int32, width)
        segment = group * group_size + local_cols // per_device
        col_label = (segment * col_devices + col_index) * per_device + local_cols % per_device
        keep = segment >= row_index
        upper = (segment != row_index)[:, None] | (row_label[None, :] < col_label[:, None])
        retain = keep[:, None] & upper & (row_label[None, :] != col_label[:, None])
        tensor = pair_tensor(pos_rows, cols_pos, retain).astype(jnp.bfloat16)
        sum_rows = sum_rows + jnp.einsum(
            "kbj,bjai->kai", cols_vec, tensor, preferred_element_type=jnp.float32
        )
        credit = jnp.einsum("kai,bjai->kbj", vec_rows, tensor, preferred_element_type=jnp.float32)
        previous = lax.dynamic_slice_in_dim(sum_cols, start, width, 2)
        sum_cols = lax.dynamic_update_slice_in_dim(sum_cols, previous + credit, start, 2)
        return (sum_rows, sum_cols)

    totals = (sum_rows, sum_cols)
    totals = lax.fori_loop(row_index // group_size, group_count, add_group, totals)
    sum_rows, sum_cols = totals
    mobility_image = own_vector + lax.psum_scatter(sum_rows, "col", scatter_dimension=2, tiled=True)
    return mobility_image + lax.psum_scatter(sum_cols, "row", scatter_dimension=2, tiled=True)


def on_device(positions, thermal_noise):
    squares = lax.psum(jnp.sum(thermal_noise * thermal_noise, axis=(1, 2)), ("row", "col"))
    noise_length = jnp.sqrt(squares + 1e-06)
    basis_one = thermal_noise / noise_length[:, None, None]
    pos_cols, cols_one = (
        lax.all_gather(positions, "row", axis=1, tiled=True),
        lax.all_gather(basis_one, "row", axis=2, tiled=True),
    )
    pos_rows, rows_wide = (
        lax.all_gather(positions, "col", axis=1, tiled=True),
        lax.all_gather(basis_one, "col", axis=2, tiled=True),
    )
    image_one = half_image(
        pos_rows, pos_cols, rows_wide.astype(jnp.bfloat16), cols_one.astype(jnp.bfloat16), basis_one
    )
    alpha_one = lax.psum(jnp.sum(basis_one * image_one, axis=(1, 2)), ("row", "col"))
    remainder = image_one - alpha_one[:, None, None] * basis_one
    beta_squared = lax.psum(jnp.sum(remainder * remainder, axis=(1, 2)), ("row", "col"))
    beta_one = jnp.sqrt(beta_squared + 1e-06)
    basis_two = remainder / beta_one[:, None, None]
    narrow_two = basis_two.astype(jnp.bfloat16)
    cols_two = lax.all_gather(narrow_two, "row", axis=2, tiled=True)
    rows_two = lax.all_gather(narrow_two, "col", axis=2, tiled=True)
    image_two = half_image(pos_rows, pos_cols, rows_two, cols_two, basis_two)
    alpha_two = lax.psum(jnp.sum(basis_two * image_two, axis=(1, 2)), ("row", "col"))
    det_root = jnp.sqrt(alpha_one * alpha_two - beta_one * beta_one)
    trace_root = jnp.sqrt(alpha_one + alpha_two + 2.0 * det_root)
    weight_one = (alpha_one + det_root) / trace_root
    weight_two = beta_one / trace_root
    return (
        0.5
        * noise_length[:, None, None]
        * (weight_one[:, None, None] * basis_one + weight_two[:, None, None] * basis_two)
    )


def solution(mesh):
    specs = dict(
        mesh=mesh,
        in_specs=(P(None, ("row", "col")), P(None, None, ("row", "col"))),
        out_specs=P(None, None, ("row", "col")),
        check_vma=False,
    )

    def program(positions, thermal_noise):
        if fits(mesh, positions, thermal_noise):
            body = functools.partial(replicated, mesh)
        else:
            body = on_device
        return jax.shard_map(body, **specs)(positions, thermal_noise)

    return program
```

```python
import functools

import jax
import jax.numpy as jnp
from jax import lax
from jax.experimental import pallas as pl
from jax.experimental.pallas import tpu as pltpu
from jax.sharding import PartitionSpec as P

LANES = 128
MESH = pl.DeviceIdType.MESH
BLOCKS = ((0, 0), (1, 1), (2, 2), (0, 1), (0, 2), (1, 2))


def partner(place, k, size):
    result = 0
    bit = 1
    while bit < size:
        digit = lax.rem(place // bit, 2)
        result = result + bit * (1 - digit if k & bit else digit)
        bit = 2 * bit
    return result


def replicated_kernel(
    rows,
    outer,
    inner,
    noise_ref,
    pos_ref,
    out_ref,
    gathered,
    stage,
    own_ref,
    noise_full,
    pos_cols,
    pos_rows,
    mobility,
    weights,
    image,
    send_line,
    recv_line,
    send_plane,
    recv_plane,
):
    _, per_device, samples = noise_ref.shape
    particles = rows * outer * inner * per_device
    f32, bf16 = jnp.float32, jnp.bfloat16
    my_row, my_col = lax.axis_index("row"), lax.axis_index("col")

    my_outer, my_inner = my_col // inner, lax.rem(my_col, inner)
    line = [partner(my_outer, k, outer) for k in range(outer)]
    plane = [
        (partner(my_row, j, rows), partner(my_inner, i, inner))
        for i in range(inner)
        for j in range(rows)
    ]

    barrier = pltpu.get_barrier_semaphore()
    for place in line[1:]:
        pl.semaphore_signal(
            barrier, inc=1, device_id=(my_row, place * inner + my_inner), device_id_type=MESH
        )
    for row, place in plane[1:]:
        pl.semaphore_signal(
            barrier, inc=1, device_id=(row, my_outer * inner + place), device_id_type=MESH
        )

    stage[...] = jnp.zeros_like(stage)
    position = pos_ref[...]
    for term in range(3):
        piece = position.astype(bf16).astype(f32)
        stage[pl.ds(3 * term, 3), pl.ds(0, per_device)] = piece
        position = position - piece
    turned = jnp.transpose(stage[...])
    own_ref[...] = jnp.zeros_like(own_ref)
    for b in range(3):
        own_ref[:, pl.ds(b * samples, samples)] = noise_ref[b]
    own_ref[:, pl.ds(3 * samples, 16)] = turned[0:per_device, :]
    own = own_ref[...]
    gathered[0, 0] = own.astype(bf16)

    pl.semaphore_wait(barrier, len(line) + len(plane) - 2)

    def line_copy(k):
        return pltpu.make_async_remote_copy(
            src_ref=gathered.at[0, 0],
            dst_ref=gathered.at[0, k],
            send_sem=send_line.at[k],
            recv_sem=recv_line.at[k],
            device_id=(my_row, line[k] * inner + my_inner),
            device_id_type=MESH,
        )

    def plane_copy(block, k):
        return pltpu.make_async_remote_copy(
            src_ref=gathered.at[0, block],
            dst_ref=gathered.at[k, block],
            send_sem=send_plane.at[k],
            recv_sem=recv_plane.at[k],
            device_id=(plane[k][0], my_outer * inner + plane[k][1]),
            device_id_type=MESH,
        )

    def finished(ref, semaphore):
        pltpu.make_async_copy(ref, ref, semaphore).wait()

    for k in range(outer - 1, 0, -1):
        line_copy(k).start()
    for k in range(1, len(plane)):
        plane_copy(0, k).start()
    for block in range(1, outer):
        finished(gathered.at[0, block], recv_line.at[block])
        for k in range(1, len(plane)):
            plane_copy(block, k).start()

    lane = lax.broadcasted_iota(jnp.int32, (1, LANES), 1)
    field = lax.broadcasted_iota(jnp.int32, (LANES, 3 * LANES), 0) - 3 * samples
    target = lax.broadcasted_iota(jnp.int32, (LANES, 3 * LANES), 1) // LANES
    select = (field == target) | (field == target + 3) | (field == target + 6)
    over_lanes = select.astype(f32).astype(bf16)
    field = lax.broadcasted_iota(jnp.int32, (3 * 16, LANES), 1) - 3 * samples
    target = lax.broadcasted_iota(jnp.int32, (3 * 16, LANES), 0) // 16
    select = (field == target) | (field == target + 3) | (field == target + 6)
    over_rows = select.astype(f32).astype(bf16)
    tiles = particles // LANES

    def form(start, tile, on_diagonal):
        at_rows = pl.ds(start, 16)
        d = [
            pos_cols[at_rows, pl.ds(a * LANES, LANES)]
            - pos_rows[pl.ds(a * 16, 16), pl.ds(tile * LANES, LANES)]
            for a in range(3)
        ]
        q = d[0] * d[0] + d[1] * d[1] + d[2] * d[2]
        if on_diagonal:
            row_label = start + lax.broadcasted_iota(jnp.int32, (16, LANES), 0)
            col_label = tile * LANES + lax.broadcasted_iota(jnp.int32, (16, LANES), 1)
            retain = row_label != col_label
            q = jnp.where(retain, q, 4.0)
        u = lax.rsqrt(q)
        r = q * u
        near = r < 2.0
        u2 = u * u
        f = jnp.where(near, 1.0 - 0.28125 * r, u * (0.75 + 0.5 * u2))
        if on_diagonal:
            f = jnp.where(retain, f, 0.0)
        h = u * jnp.where(near, 0.09375, u2 * (0.75 - 1.5 * u2))
        hd = [h * d[a] for a in range(3)]
        for n, (a, b) in enumerate(BLOCKS):
            element = hd[a] * d[b]
            if a == b:
                element = element + f
            mobility[n * tiles + tile, at_rows, :] = element.astype(bf16)

    per_tile = LANES // (outer * per_device)
    for tile in range(tiles):
        for k in range(tile * per_tile, (tile + 1) * per_tile):
            if k:
                finished(gathered.at[k], recv_plane.at[k])
        packed = gathered[pl.ds(tile * per_tile, per_tile)].reshape(LANES, LANES)
        pos_cols[pl.ds(tile * LANES, LANES), :] = jnp.dot(
            packed, over_lanes, preferred_element_type=f32
        )
        pos_rows[:, pl.ds(tile * LANES, LANES)] = lax.dot_general(
            over_rows, packed, (((1,), (1,)), ((), ())), preferred_element_type=f32
        )

        @pl.loop(0, LANES // 16)
        def _(step, tile=tile):
            for other in range(tile + 1):
                start = pl.multiple_of(tile * LANES + step * 16, 16)
                form(start, other, other == tile)
            for other in range(tile):
                start = pl.multiple_of(other * LANES + step * 16, 16)
                form(start, tile, False)

    group = lane // samples

    def set_weights(start, x):
        down = pltpu.roll(x, LANES - samples, 1)
        up = pltpu.roll(x, samples, 1)
        across = pltpu.roll(x, 2 * samples, 1)
        moved = {
            (0, 0): jnp.where(group == 0, x, 0.0),
            (1, 1): jnp.where(group == 1, x, 0.0),
            (2, 2): jnp.where(group == 2, x, 0.0),
            (0, 1): jnp.where(group == 0, down, jnp.where(group == 1, up, 0.0)),
            (1, 2): jnp.where(group == 1, down, jnp.where(group == 2, up, 0.0)),
            (0, 2): jnp.where((group == 0) | (group == 2), across, 0.0),
        }
        for n, pair in enumerate(BLOCKS):
            weights[pl.ds(n * particles + start, x.shape[0]), :] = moved[pair].astype(bf16)

    def fold(x):
        return jnp.sum(x.reshape(-1, 8, LANES), axis=0)

    def total(x):
        row = jnp.broadcast_to(jnp.sum(x, axis=0, keepdims=True), (8, LANES))
        row = row + pltpu.roll(row, 2 * samples, 1)
        row = row + pltpu.roll(row, samples, 1)
        return row[0:1, :]

    step_rows = 64

    def sweep(function):
        def step(index, partial):
            start = index * step_rows
            return partial + function(start, pl.ds(start, step_rows))

        partial = jnp.zeros((8, LANES), f32)
        for index in range(particles // step_rows):
            partial = step(index, partial)
        return total(partial)

    def product(row_tiles, col_tiles):
        at_rows = pl.ds(row_tiles[0] * LANES, len(row_tiles) * LANES)
        first, count = col_tiles[0], len(col_tiles)
        left = jnp.concatenate(
            [mobility[n * tiles + first + t, at_rows, :] for n in range(6) for t in range(count)],
            axis=1,
        )
        right = jnp.concatenate(
            [
                weights[pl.ds(n * particles + first * LANES, count * LANES), :]
                for n in range(6)
            ],
            axis=0,
        )
        return jnp.dot(left, right, preferred_element_type=f32)

    is_noise = lane < 3 * samples
    at_own = pl.ds(0, per_device)
    low, high = list(range(tiles // 2)), list(range(tiles // 2, tiles))
    at_low, at_high = pl.ds(0, particles // 2), pl.ds(particles // 2, particles // 2)
    for tile in range(tiles):
        wide = gathered[pl.ds(tile * per_tile, per_tile)].reshape(LANES, LANES).astype(f32)
        noise_full[pl.ds(tile * LANES, LANES), :] = jnp.where(is_noise, wide, 0.0)
        set_weights(tile * LANES, wide)
    noise_full[at_own, :] = jnp.where(is_noise, own_ref[...], 0.0)

    def noise_square(start, at):
        return fold(noise_full[at, :] * noise_full[at, :])

    length = jnp.sqrt(sweep(noise_square) + 1e-06)
    inverse = 1.0 / length
    image[at_low, :] = product(low, low + high)
    image[at_high, :] = product(high, low + high)


    def first_quotient(start, at):
        basis_one = noise_full[at, :] * inverse
        image_one = basis_one + image[at, :] * inverse
        noise_full[at, :] = basis_one
        image[at, :] = image_one
        return fold(basis_one * image_one)

    alpha_one = sweep(first_quotient)

    def remainder_square(start, at):
        remainder = image[at, :] - alpha_one * noise_full[at, :]
        image[at, :] = remainder
        return fold(remainder * remainder)

    beta_one = jnp.sqrt(sweep(remainder_square) + 1e-06)
    inverse_beta = 1.0 / beta_one

    def second_basis(start, at):
        basis_two = image[at, :] * inverse_beta
        image[at, :] = basis_two
        set_weights(start, basis_two)
        return fold(basis_two * basis_two)

    alpha_two = sweep(second_basis)
    alpha_two = alpha_two + total(
        fold(image[at_low, :] * product(low, low))
        + 2.0 * fold(image[at_low, :] * product(low, high))
        + fold(image[at_high, :] * product(high, high))
    )
    det_root = jnp.sqrt(alpha_one * alpha_two - beta_one * beta_one)
    trace_root = jnp.sqrt(alpha_one + alpha_two + 2.0 * det_root)
    weight_one = (alpha_one + det_root) / trace_root
    weight_two = beta_one / trace_root
    result = 0.5 * length * (weight_one * noise_full[at_own, :] + weight_two * image[at_own, :])
    for b in range(3):
        out_ref[b] = result[:, b * samples : (b + 1) * samples]

    for k in range(1, outer):
        line_copy(k).wait_send()
    for k in range(1, len(plane)):
        finished(gathered.at[0], send_plane.at[k])


def replicated(mesh, positions, thermal_noise):
    rows, cols = mesh.shape["row"], mesh.shape["col"]
    samples, _, per_device = thermal_noise.shape
    particles = rows * cols * per_device
    inner = 2 if cols % 2 == 0 else 1
    outer = cols // inner
    f32, bf16 = jnp.float32, jnp.bfloat16
    vmem = pl.BlockSpec(memory_space=pltpu.VMEM)
    out = pl.pallas_call(
        functools.partial(replicated_kernel, rows, outer, inner),
        out_shape=jax.ShapeDtypeStruct((3, per_device, samples), f32),
        in_specs=[vmem, vmem],
        out_specs=vmem,
        scratch_shapes=[
            pltpu.VMEM((rows * inner, outer, per_device, LANES), bf16),
            pltpu.VMEM((16, LANES), f32),
            pltpu.VMEM((per_device, LANES), f32),
            pltpu.VMEM((particles, LANES), f32),
            pltpu.VMEM((particles, 3 * LANES), f32),
            pltpu.VMEM((3 * 16, particles), f32),
            pltpu.VMEM((6 * particles // LANES, particles, LANES), bf16),
            pltpu.VMEM((6 * particles, LANES), bf16),
            pltpu.VMEM((particles, LANES), f32),
            pltpu.SemaphoreType.DMA((outer,)),
            pltpu.SemaphoreType.DMA((outer,)),
            pltpu.SemaphoreType.DMA((rows * inner,)),
            pltpu.SemaphoreType.DMA((rows * inner,)),
        ],
        compiler_params=pltpu.CompilerParams(collective_id=0, has_side_effects=True),
        name="lanczos",
    )(jnp.transpose(thermal_noise, (1, 2, 0)), positions)
    return jnp.transpose(out, (2, 0, 1))


def fits(mesh, positions, thermal_noise):
    rows, cols = mesh.shape["row"], mesh.shape["col"]
    samples, _, particles = thermal_noise.shape
    per_device = particles // (rows * cols)
    outer = cols // 2 if cols % 2 == 0 else cols
    return (
        rows & (rows - 1) == 0
        and cols & (cols - 1) == 0
        and 4 * samples == LANES
        and per_device % 16 == 0
        and LANES % (outer * per_device) == 0
        and particles % (2 * LANES) == 0
        and 12 * particles * particles <= 2**24
    )


def pair_tensor(rows_pos, cols_pos, retain):
    offsets = [rows_pos[a][None, :] - cols_pos[a][:, None] for a in range(3)]
    squared = offsets[0] * offsets[0] + offsets[1] * offsets[1] + offsets[2] * offsets[2]
    guarded = jnp.where(retain, squared, 4.0)
    inverse = lax.rsqrt(guarded)
    distance = guarded * inverse
    correlation = distance < 2.0
    inverse_cube = inverse * inverse * inverse
    inverse_fifth = inverse_cube * inverse * inverse
    isotropic = jnp.where(
        correlation, 1.0 - 0.28125 * distance, 0.75 * inverse + 0.5 * inverse_cube
    )
    dyadic = jnp.where(correlation, 0.09375 * inverse, 0.75 * inverse_cube - 1.5 * inverse_fifth)
    isotropic = jnp.where(retain, isotropic, 0.0)
    dyadic = jnp.where(retain, dyadic, 0.0)
    columns = []
    for b in range(3):
        elements = []
        for a in range(3):
            element = dyadic * offsets[a] * offsets[b]
            if a == b:
                element = element + isotropic
            elements.append(element)
        columns.append(jnp.stack(elements, axis=1))
    return jnp.stack(columns, axis=0)


def half_image(pos_rows, pos_cols, vec_rows, vec_cols, own_vector):
    row_devices = lax.axis_size("row")
    col_devices = lax.axis_size("col")
    row_index = lax.axis_index("row")
    col_index = lax.axis_index("col")
    samples = own_vector.shape[0]
    per_device = own_vector.shape[2]
    row_count = pos_rows.shape[1]
    row_label = row_index * col_devices * per_device + lax.iota(jnp.int32, row_count)
    group_size = min(row_devices, max(1, 128 // per_device))
    width = group_size * per_device
    group_count = row_devices // group_size
    sum_rows = jnp.zeros((samples, 3, row_count), jnp.float32)
    sum_cols = jnp.zeros((samples, 3, per_device * row_devices), jnp.float32)

    def add_group(group, totals):
        sum_rows, sum_cols = totals
        start = group * width
        cols_pos = lax.dynamic_slice_in_dim(pos_cols, start, width, 1)
        cols_vec = lax.dynamic_slice_in_dim(vec_cols, start, width, 2)
        local_cols = lax.iota(jnp.int32, width)
        segment = group * group_size + local_cols // per_device
        col_label = (segment * col_devices + col_index) * per_device + local_cols % per_device
        keep = segment >= row_index
        upper = (segment != row_index)[:, None] | (row_label[None, :] < col_label[:, None])
        retain = keep[:, None] & upper & (row_label[None, :] != col_label[:, None])
        tensor = pair_tensor(pos_rows, cols_pos, retain).astype(jnp.bfloat16)
        sum_rows = sum_rows + jnp.einsum(
            "kbj,bjai->kai", cols_vec, tensor, preferred_element_type=jnp.float32
        )
        credit = jnp.einsum("kai,bjai->kbj", vec_rows, tensor, preferred_element_type=jnp.float32)
        previous = lax.dynamic_slice_in_dim(sum_cols, start, width, 2)
        sum_cols = lax.dynamic_update_slice_in_dim(sum_cols, previous + credit, start, 2)
        return (sum_rows, sum_cols)

    totals = (sum_rows, sum_cols)
    totals = lax.fori_loop(row_index // group_size, group_count, add_group, totals)
    sum_rows, sum_cols = totals
    mobility_image = own_vector + lax.psum_scatter(sum_rows, "col", scatter_dimension=2, tiled=True)
    return mobility_image + lax.psum_scatter(sum_cols, "row", scatter_dimension=2, tiled=True)


def on_device(positions, thermal_noise):
    squares = lax.psum(jnp.sum(thermal_noise * thermal_noise, axis=(1, 2)), ("row", "col"))
    noise_length = jnp.sqrt(squares + 1e-06)
    basis_one = thermal_noise / noise_length[:, None, None]
    pos_cols, cols_one = (
        lax.all_gather(positions, "row", axis=1, tiled=True),
        lax.all_gather(basis_one, "row", axis=2, tiled=True),
    )
    pos_rows, rows_wide = (
        lax.all_gather(positions, "col", axis=1, tiled=True),
        lax.all_gather(basis_one, "col", axis=2, tiled=True),
    )
    image_one = half_image(
        pos_rows, pos_cols, rows_wide.astype(jnp.bfloat16), cols_one.astype(jnp.bfloat16), basis_one
    )
    alpha_one = lax.psum(jnp.sum(basis_one * image_one, axis=(1, 2)), ("row", "col"))
    remainder = image_one - alpha_one[:, None, None] * basis_one
    beta_squared = lax.psum(jnp.sum(remainder * remainder, axis=(1, 2)), ("row", "col"))
    beta_one = jnp.sqrt(beta_squared + 1e-06)
    basis_two = remainder / beta_one[:, None, None]
    narrow_two = basis_two.astype(jnp.bfloat16)
    cols_two = lax.all_gather(narrow_two, "row", axis=2, tiled=True)
    rows_two = lax.all_gather(narrow_two, "col", axis=2, tiled=True)
    image_two = half_image(pos_rows, pos_cols, rows_two, cols_two, basis_two)
    alpha_two = lax.psum(jnp.sum(basis_two * image_two, axis=(1, 2)), ("row", "col"))
    det_root = jnp.sqrt(alpha_one * alpha_two - beta_one * beta_one)
    trace_root = jnp.sqrt(alpha_one + alpha_two + 2.0 * det_root)
    weight_one = (alpha_one + det_root) / trace_root
    weight_two = beta_one / trace_root
    return (
        0.5
        * noise_length[:, None, None]
        * (weight_one[:, None, None] * basis_one + weight_two[:, None, None] * basis_two)
    )


def solution(mesh):
    specs = dict(
        mesh=mesh,
        in_specs=(P(None, ("row", "col")), P(None, None, ("row", "col"))),
        out_specs=P(None, None, ("row", "col")),
        check_vma=False,
    )

    def program(positions, thermal_noise):
        if fits(mesh, positions, thermal_noise):
            body = functools.partial(replicated, mesh)
        else:
            body = on_device
        return jax.shard_map(body, **specs)(positions, thermal_noise)

    return program
```

```python
import functools

import jax
import jax.numpy as jnp
from jax import lax
from jax.experimental import pallas as pl
from jax.experimental.pallas import tpu as pltpu
from jax.sharding import PartitionSpec as P

LANES = 128
MESH = pl.DeviceIdType.MESH
BLOCKS = ((0, 0), (1, 1), (2, 2), (0, 1), (0, 2), (1, 2))


def partner(place, k, size):
    result = 0
    bit = 1
    while bit < size:
        digit = lax.rem(place // bit, 2)
        result = result + bit * (1 - digit if k & bit else digit)
        bit = 2 * bit
    return result


def replicated_kernel(
    rows,
    outer,
    inner,
    noise_ref,
    pos_ref,
    out_ref,
    gathered,
    stage,
    own_ref,
    noise_full,
    pos_cols,
    pos_rows,
    mobility,
    weights,
    image,
    send_line,
    recv_line,
    send_plane,
    recv_plane,
):
    _, per_device, samples = noise_ref.shape
    particles = rows * outer * inner * per_device
    f32, bf16 = jnp.float32, jnp.bfloat16
    my_row, my_col = lax.axis_index("row"), lax.axis_index("col")

    my_outer, my_inner = my_col // inner, lax.rem(my_col, inner)
    line = [partner(my_outer, k, outer) for k in range(outer)]
    plane = [
        (partner(my_row, j, rows), partner(my_inner, i, inner))
        for i in range(inner)
        for j in range(rows)
    ]

    barrier = pltpu.get_barrier_semaphore()
    for place in line[1:]:
        pl.semaphore_signal(
            barrier, inc=1, device_id=(my_row, place * inner + my_inner), device_id_type=MESH
        )
    for row, place in plane[1:]:
        pl.semaphore_signal(
            barrier, inc=1, device_id=(row, my_outer * inner + place), device_id_type=MESH
        )

    stage[...] = jnp.zeros_like(stage)
    position = pos_ref[...]
    for term in range(3):
        piece = position.astype(bf16).astype(f32)
        stage[pl.ds(3 * term, 3), pl.ds(0, per_device)] = piece
        position = position - piece
    turned = jnp.transpose(stage[...])
    own_ref[...] = jnp.zeros_like(own_ref)
    for b in range(3):
        own_ref[:, pl.ds(b * samples, samples)] = noise_ref[b]
    own_ref[:, pl.ds(3 * samples, 16)] = turned[0:per_device, :]
    own = own_ref[...]
    gathered[0, 0] = own.astype(bf16)

    pl.semaphore_wait(barrier, len(line) + len(plane) - 2)

    def line_copy(k):
        return pltpu.make_async_remote_copy(
            src_ref=gathered.at[0, 0],
            dst_ref=gathered.at[0, k],
            send_sem=send_line.at[k],
            recv_sem=recv_line.at[k],
            device_id=(my_row, line[k] * inner + my_inner),
            device_id_type=MESH,
        )

    def plane_copy(block, k):
        return pltpu.make_async_remote_copy(
            src_ref=gathered.at[0, block],
            dst_ref=gathered.at[k, block],
            send_sem=send_plane.at[k],
            recv_sem=recv_plane.at[k],
            device_id=(plane[k][0], my_outer * inner + plane[k][1]),
            device_id_type=MESH,
        )

    def finished(ref, semaphore):
        pltpu.make_async_copy(ref, ref, semaphore).wait()

    for k in range(outer - 1, 0, -1):
        line_copy(k).start()
    for k in range(1, len(plane)):
        plane_copy(0, k).start()
    for block in range(1, outer):
        finished(gathered.at[0, block], recv_line.at[block])
        for k in range(1, len(plane)):
            plane_copy(block, k).start()

    lane = lax.broadcasted_iota(jnp.int32, (1, LANES), 1)
    field = lax.broadcasted_iota(jnp.int32, (LANES, 3 * LANES), 0) - 3 * samples
    target = lax.broadcasted_iota(jnp.int32, (LANES, 3 * LANES), 1) // LANES
    select = (field == target) | (field == target + 3) | (field == target + 6)
    over_lanes = select.astype(f32).astype(bf16)
    field = lax.broadcasted_iota(jnp.int32, (3 * 16, LANES), 1) - 3 * samples
    target = lax.broadcasted_iota(jnp.int32, (3 * 16, LANES), 0) // 16
    select = (field == target) | (field == target + 3) | (field == target + 6)
    over_rows = select.astype(f32).astype(bf16)
    tiles = particles // LANES

    def form(start, tile, on_diagonal):
        at_rows = pl.ds(start, 16)
        d = [
            pos_cols[at_rows, pl.ds(a * LANES, LANES)]
            - pos_rows[pl.ds(a * 16, 16), pl.ds(tile * LANES, LANES)]
            for a in range(3)
        ]
        q = d[0] * d[0] + d[1] * d[1] + d[2] * d[2]
        if on_diagonal:
            row_label = start + lax.broadcasted_iota(jnp.int32, (16, LANES), 0)
            col_label = tile * LANES + lax.broadcasted_iota(jnp.int32, (16, LANES), 1)
            retain = row_label != col_label
            q = jnp.where(retain, q, 4.0)
        u = lax.rsqrt(q)
        r = q * u
        near = r < 2.0
        u2 = u * u
        f = jnp.where(near, 1.0 - 0.28125 * r, u * (0.75 + 0.5 * u2))
        if on_diagonal:
            f = jnp.where(retain, f, 0.0)
        h = u * jnp.where(near, 0.09375, u2 * (0.75 - 1.5 * u2))
        hd = [h * d[a] for a in range(3)]
        for n, (a, b) in enumerate(BLOCKS):
            element = hd[a] * d[b]
            if a == b:
                element = element + f
            mobility[n * tiles + tile, at_rows, :] = element.astype(bf16)

    group = lane // samples

    def set_weights(start, x):
        down = pltpu.roll(x, LANES - samples, 1)
        up = pltpu.roll(x, samples, 1)
        across = pltpu.roll(x, 2 * samples, 1)
        moved = {
            (0, 0): jnp.where(group == 0, x, 0.0),
            (1, 1): jnp.where(group == 1, x, 0.0),
            (2, 2): jnp.where(group == 2, x, 0.0),
            (0, 1): jnp.where(group == 0, down, jnp.where(group == 1, up, 0.0)),
            (1, 2): jnp.where(group == 1, down, jnp.where(group == 2, up, 0.0)),
            (0, 2): jnp.where((group == 0) | (group == 2), across, 0.0),
        }
        for n, pair in enumerate(BLOCKS):
            weights[pl.ds(n * particles + start, x.shape[0]), :] = moved[pair].astype(bf16)

    def fold(x):
        return jnp.sum(x.reshape(-1, 8, LANES), axis=0)

    def total(x):
        row = jnp.broadcast_to(jnp.sum(x, axis=0, keepdims=True), (8, LANES))
        row = row + pltpu.roll(row, 2 * samples, 1)
        row = row + pltpu.roll(row, samples, 1)
        return row[0:1, :]

    step_rows = 64

    def sweep(function):
        def step(index, partial):
            start = index * step_rows
            return partial + function(start, pl.ds(start, step_rows))

        partial = jnp.zeros((8, LANES), f32)
        for index in range(particles // step_rows):
            partial = step(index, partial)
        return total(partial)

    def product(row_tiles, col_tiles):
        at_rows = pl.ds(row_tiles[0] * LANES, len(row_tiles) * LANES)
        first, count = col_tiles[0], len(col_tiles)
        left = jnp.concatenate(
            [mobility[n * tiles + first + t, at_rows, :] for n in range(6) for t in range(count)],
            axis=1,
        )
        right = jnp.concatenate(
            [
                weights[pl.ds(n * particles + first * LANES, count * LANES), :]
                for n in range(6)
            ],
            axis=0,
        )
        return jnp.dot(left, right, preferred_element_type=f32)

    is_noise = lane < 3 * samples
    at_own = pl.ds(0, per_device)
    low, high = list(range(tiles // 2)), list(range(tiles // 2, tiles))
    early, late = list(range(tiles // 2)), list(range(tiles // 2, tiles))
    at_low, at_high = pl.ds(0, particles // 2), pl.ds(particles // 2, particles // 2)
    at_early, at_late = pl.ds(0, len(early) * LANES), pl.ds(len(early) * LANES, len(late) * LANES)
    per_tile = LANES // (outer * per_device)
    for tile in range(tiles):
        for k in range(tile * per_tile, (tile + 1) * per_tile):
            if k:
                finished(gathered.at[k], recv_plane.at[k])
        packed = gathered[pl.ds(tile * per_tile, per_tile)].reshape(LANES, LANES)
        pos_cols[pl.ds(tile * LANES, LANES), :] = jnp.dot(
            packed, over_lanes, preferred_element_type=f32
        )
        pos_rows[:, pl.ds(tile * LANES, LANES)] = lax.dot_general(
            over_rows, packed, (((1,), (1,)), ((), ())), preferred_element_type=f32
        )

        wide = packed.astype(f32)
        noise_full[pl.ds(tile * LANES, LANES), :] = jnp.where(is_noise, wide, 0.0)
        set_weights(tile * LANES, wide)

        if tile == tiles - 1:
            image[pl.ds(0, len(early) * LANES), :] = product(early, low)
            for step in range(LANES // 16):
                for other in range(tile + 1):
                    form(tile * LANES + step * 16, other, other == tile)
                for other in range(tile):
                    form(other * LANES + step * 16, tile, False)
        else:

            @pl.loop(0, LANES // 16)
            def _(step, tile=tile):
                for other in range(tile + 1):
                    start = pl.multiple_of(tile * LANES + step * 16, 16)
                    form(start, other, other == tile)
                for other in range(tile):
                    start = pl.multiple_of(other * LANES + step * 16, 16)
                    form(start, tile, False)

    noise_full[at_own, :] = jnp.where(is_noise, own_ref[...], 0.0)

    def noise_square(start, at):
        return fold(noise_full[at, :] * noise_full[at, :])

    length = jnp.sqrt(sweep(noise_square) + 1e-06)
    inverse = 1.0 / length
    image[at_early, :] = image[at_early, :] + product(early, high)
    image[at_late, :] = product(late, low + high)

    def first_quotient(start, at):
        basis_one = noise_full[at, :] * inverse
        image_one = basis_one + image[at, :] * inverse
        noise_full[at, :] = basis_one
        image[at, :] = image_one
        return fold(basis_one * image_one)

    alpha_one = sweep(first_quotient)

    def remainder_square(start, at):
        remainder = image[at, :] - alpha_one * noise_full[at, :]
        image[at, :] = remainder
        return fold(remainder * remainder)

    beta_one = jnp.sqrt(sweep(remainder_square) + 1e-06)
    inverse_beta = 1.0 / beta_one

    def second_basis(start, at):
        basis_two = image[at, :] * inverse_beta
        image[at, :] = basis_two
        set_weights(start, basis_two)
        return fold(basis_two * basis_two)

    alpha_two = sweep(second_basis)
    alpha_two = alpha_two + total(
        fold(image[at_low, :] * product(low, low))
        + 2.0 * fold(image[at_low, :] * product(low, high))
        + fold(image[at_high, :] * product(high, high))
    )
    det_root = jnp.sqrt(alpha_one * alpha_two - beta_one * beta_one)
    trace_root = jnp.sqrt(alpha_one + alpha_two + 2.0 * det_root)
    weight_one = (alpha_one + det_root) / trace_root
    weight_two = beta_one / trace_root
    result = 0.5 * length * (weight_one * noise_full[at_own, :] + weight_two * image[at_own, :])
    for b in range(3):
        out_ref[b] = result[:, b * samples : (b + 1) * samples]

    for k in range(1, outer):
        line_copy(k).wait_send()
    for k in range(1, len(plane)):
        finished(gathered.at[0], send_plane.at[k])


def replicated(mesh, positions, thermal_noise):
    rows, cols = mesh.shape["row"], mesh.shape["col"]
    samples, _, per_device = thermal_noise.shape
    particles = rows * cols * per_device
    inner = 2 if cols % 2 == 0 else 1
    outer = cols // inner
    f32, bf16 = jnp.float32, jnp.bfloat16
    vmem = pl.BlockSpec(memory_space=pltpu.VMEM)
    out = pl.pallas_call(
        functools.partial(replicated_kernel, rows, outer, inner),
        out_shape=jax.ShapeDtypeStruct((3, per_device, samples), f32),
        in_specs=[vmem, vmem],
        out_specs=vmem,
        scratch_shapes=[
            pltpu.VMEM((rows * inner, outer, per_device, LANES), bf16),
            pltpu.VMEM((16, LANES), f32),
            pltpu.VMEM((per_device, LANES), f32),
            pltpu.VMEM((particles, LANES), f32),
            pltpu.VMEM((particles, 3 * LANES), f32),
            pltpu.VMEM((3 * 16, particles), f32),
            pltpu.VMEM((6 * particles // LANES, particles, LANES), bf16),
            pltpu.VMEM((6 * particles, LANES), bf16),
            pltpu.VMEM((particles, LANES), f32),
            pltpu.SemaphoreType.DMA((outer,)),
            pltpu.SemaphoreType.DMA((outer,)),
            pltpu.SemaphoreType.DMA((rows * inner,)),
            pltpu.SemaphoreType.DMA((rows * inner,)),
        ],
        compiler_params=pltpu.CompilerParams(collective_id=0, has_side_effects=True),
        name="lanczos",
    )(jnp.transpose(thermal_noise, (1, 2, 0)), positions)
    return jnp.transpose(out, (2, 0, 1))


def fits(mesh, positions, thermal_noise):
    rows, cols = mesh.shape["row"], mesh.shape["col"]
    samples, _, particles = thermal_noise.shape
    per_device = particles // (rows * cols)
    outer = cols // 2 if cols % 2 == 0 else cols
    return (
        rows & (rows - 1) == 0
        and cols & (cols - 1) == 0
        and 4 * samples == LANES
        and per_device % 16 == 0
        and LANES % (outer * per_device) == 0
        and particles % (2 * LANES) == 0
        and 12 * particles * particles <= 2**24
    )


def pair_tensor(rows_pos, cols_pos, retain):
    offsets = [rows_pos[a][None, :] - cols_pos[a][:, None] for a in range(3)]
    squared = offsets[0] * offsets[0] + offsets[1] * offsets[1] + offsets[2] * offsets[2]
    guarded = jnp.where(retain, squared, 4.0)
    inverse = lax.rsqrt(guarded)
    distance = guarded * inverse
    correlation = distance < 2.0
    inverse_cube = inverse * inverse * inverse
    inverse_fifth = inverse_cube * inverse * inverse
    isotropic = jnp.where(
        correlation, 1.0 - 0.28125 * distance, 0.75 * inverse + 0.5 * inverse_cube
    )
    dyadic = jnp.where(correlation, 0.09375 * inverse, 0.75 * inverse_cube - 1.5 * inverse_fifth)
    isotropic = jnp.where(retain, isotropic, 0.0)
    dyadic = jnp.where(retain, dyadic, 0.0)
    columns = []
    for b in range(3):
        elements = []
        for a in range(3):
            element = dyadic * offsets[a] * offsets[b]
            if a == b:
                element = element + isotropic
            elements.append(element)
        columns.append(jnp.stack(elements, axis=1))
    return jnp.stack(columns, axis=0)


def half_image(pos_rows, pos_cols, vec_rows, vec_cols, own_vector):
    row_devices = lax.axis_size("row")
    col_devices = lax.axis_size("col")
    row_index = lax.axis_index("row")
    col_index = lax.axis_index("col")
    samples = own_vector.shape[0]
    per_device = own_vector.shape[2]
    row_count = pos_rows.shape[1]
    row_label = row_index * col_devices * per_device + lax.iota(jnp.int32, row_count)
    group_size = min(row_devices, max(1, 128 // per_device))
    width = group_size * per_device
    group_count = row_devices // group_size
    sum_rows = jnp.zeros((samples, 3, row_count), jnp.float32)
    sum_cols = jnp.zeros((samples, 3, per_device * row_devices), jnp.float32)

    def add_group(group, totals):
        sum_rows, sum_cols = totals
        start = group * width
        cols_pos = lax.dynamic_slice_in_dim(pos_cols, start, width, 1)
        cols_vec = lax.dynamic_slice_in_dim(vec_cols, start, width, 2)
        local_cols = lax.iota(jnp.int32, width)
        segment = group * group_size + local_cols // per_device
        col_label = (segment * col_devices + col_index) * per_device + local_cols % per_device
        keep = segment >= row_index
        upper = (segment != row_index)[:, None] | (row_label[None, :] < col_label[:, None])
        retain = keep[:, None] & upper & (row_label[None, :] != col_label[:, None])
        tensor = pair_tensor(pos_rows, cols_pos, retain).astype(jnp.bfloat16)
        sum_rows = sum_rows + jnp.einsum(
            "kbj,bjai->kai", cols_vec, tensor, preferred_element_type=jnp.float32
        )
        credit = jnp.einsum("kai,bjai->kbj", vec_rows, tensor, preferred_element_type=jnp.float32)
        previous = lax.dynamic_slice_in_dim(sum_cols, start, width, 2)
        sum_cols = lax.dynamic_update_slice_in_dim(sum_cols, previous + credit, start, 2)
        return (sum_rows, sum_cols)

    totals = (sum_rows, sum_cols)
    totals = lax.fori_loop(row_index // group_size, group_count, add_group, totals)
    sum_rows, sum_cols = totals
    mobility_image = own_vector + lax.psum_scatter(sum_rows, "col", scatter_dimension=2, tiled=True)
    return mobility_image + lax.psum_scatter(sum_cols, "row", scatter_dimension=2, tiled=True)


def on_device(positions, thermal_noise):
    squares = lax.psum(jnp.sum(thermal_noise * thermal_noise, axis=(1, 2)), ("row", "col"))
    noise_length = jnp.sqrt(squares + 1e-06)
    basis_one = thermal_noise / noise_length[:, None, None]
    pos_cols, cols_one = (
        lax.all_gather(positions, "row", axis=1, tiled=True),
        lax.all_gather(basis_one, "row", axis=2, tiled=True),
    )
    pos_rows, rows_wide = (
        lax.all_gather(positions, "col", axis=1, tiled=True),
        lax.all_gather(basis_one, "col", axis=2, tiled=True),
    )
    image_one = half_image(
        pos_rows, pos_cols, rows_wide.astype(jnp.bfloat16), cols_one.astype(jnp.bfloat16), basis_one
    )
    alpha_one = lax.psum(jnp.sum(basis_one * image_one, axis=(1, 2)), ("row", "col"))
    remainder = image_one - alpha_one[:, None, None] * basis_one
    beta_squared = lax.psum(jnp.sum(remainder * remainder, axis=(1, 2)), ("row", "col"))
    beta_one = jnp.sqrt(beta_squared + 1e-06)
    basis_two = remainder / beta_one[:, None, None]
    narrow_two = basis_two.astype(jnp.bfloat16)
    cols_two = lax.all_gather(narrow_two, "row", axis=2, tiled=True)
    rows_two = lax.all_gather(narrow_two, "col", axis=2, tiled=True)
    image_two = half_image(pos_rows, pos_cols, rows_two, cols_two, basis_two)
    alpha_two = lax.psum(jnp.sum(basis_two * image_two, axis=(1, 2)), ("row", "col"))
    det_root = jnp.sqrt(alpha_one * alpha_two - beta_one * beta_one)
    trace_root = jnp.sqrt(alpha_one + alpha_two + 2.0 * det_root)
    weight_one = (alpha_one + det_root) / trace_root
    weight_two = beta_one / trace_root
    return (
        0.5
        * noise_length[:, None, None]
        * (weight_one[:, None, None] * basis_one + weight_two[:, None, None] * basis_two)
    )


def solution(mesh):
    specs = dict(
        mesh=mesh,
        in_specs=(P(None, ("row", "col")), P(None, None, ("row", "col"))),
        out_specs=P(None, None, ("row", "col")),
        check_vma=False,
    )

    def program(positions, thermal_noise):
        if fits(mesh, positions, thermal_noise):
            body = functools.partial(replicated, mesh)
        else:
            body = on_device
        return jax.shard_map(body, **specs)(positions, thermal_noise)

    return program
```
